32 devices in a mesh: group: 2 (over y), ctx: 4 (over x, core), tp: 4 (over z).
Axes of the slice: x: 2, y: 2, z: 4, core: 2. Of those that a mesh axis runs over, the one named last changes fastest.
Arguments:
- x_in: bfloat16 [4096, 16384], P(('group', 'ctx'), 'tp'), parts along dimension 0, may hold values from -6 to 6
- bc_in: bfloat16 [4096, 2, 2048], P(('group', 'ctx'), None, 'tp'), parts along dimension 0, may hold values from -6 to 6
- z_in: bfloat16 [4096, 16384], P(('group', 'ctx'), 'tp'), parts along dimension 0, may hold values from -6 to 6
- dt_raw: float32 [4096, 256], P(('group', 'ctx'), 'tp'), parts along dimension 0, may hold values from -3 to 3
- conv_x: bfloat16 [4, 16384], P(None, 'tp'), may hold values from -3 to 3
- conv_bc: bfloat16 [4, 2, 2048], P(None, None, 'tp'), may hold values from -3 to 3
- conv_bias_x: float32 [16384], P('tp'), may hold values from -0.9 to -0.1
- conv_bias_bc: float32 [2, 2048], P(None, 'tp'), may hold values from -0.9 to -0.1
- dt_bias: float32 [256], P('tp'), may hold values from -12 to 2
- a_log: float32 [256], P('tp'), may hold values from -12 to 4
- d_skip: float32 [256], P('tp'), may hold values from 0.5 to 2
- norm_gain: float32 [16384], P('tp'), may hold values from 0.5 to 1.5
Outputs:
- mixed: bfloat16 [4096, 16384], P(('group', 'ctx'), 'tp'), parts along dimension 0
- final_state: float32 [512, 64, 256], P(('group', 'tp'), None, 'ctx'), parts along dimension 0
The draws below stay inside these ranges and needn't reach their ends.
There are 2 independent parts, one for each index of `group`. The reference program is written for one: setup_inputs(seed, part) draws one part's arguments, and reference() takes and returns one part's arrays. A program takes and returns all parts, laid end to end along the dimension named above; an argument that names none is the same for every part. Nothing has to cross between parts.
All inputs are finite; a program needn't handle non-finite values.
Results may differ from the reference program's by a relative error of at most 0.0059.
Values may be sent and summed in bfloat16 or wider, within the bound.
A program may use at most 192 MiB of HBM per device.

```python
import jax
import jax.numpy as jnp
from jax import lax

HEADS = 256
HEAD_DIM = 64
STATE = 256
GROUPS = 8
KERNEL = 4
SPAN = 128
TOK_DEV = 512
TOKENS = 2048


def head_law(key):
    stream = jax.random.fold_in(key, 7)
    pick_key, slow_key, middle_key, fast_key = jax.random.split(stream, 4)
    slow_share = 0.5
    middle_share = 0.35
    picker = jax.random.uniform(pick_key, (HEADS,), jnp.float32)
    slow_mask = picker < slow_share
    middle_mask = picker < slow_share + middle_share
    slow_rate = jnp.exp(jax.random.uniform(slow_key, (HEADS,), jnp.float32, jnp.log(0.15), jnp.log(0.8))) / TOKENS
    middle_rate = jax.random.uniform(middle_key, (HEADS,), jnp.float32, 0.8, 1.5) / SPAN
    fast_rate = jax.random.uniform(fast_key, (HEADS,), jnp.float32, 8.0, 12.0) / SPAN
    fade_rate = jnp.where(slow_mask, slow_rate, jnp.where(middle_mask, middle_rate, fast_rate))
    window = 0.5 / fade_rate
    mean_step = 0.25 / (0.006 * window + 0.16 * jnp.sqrt(window) + 1.0)
    return (fade_rate, mean_step)


def draw_a_log(key, part):
    fade_rate, mean_step = head_law(key)
    return jnp.log(fade_rate / mean_step)


def draw_dt_bias(key, part):
    fade_rate, mean_step = head_law(key)
    return jnp.log(jnp.expm1(mean_step))


def draw_dt_raw(key, part):
    noise_key, offset_key = jax.random.split(jax.random.fold_in(key, 3))
    jitter = jnp.clip(0.7 * jax.random.normal(noise_key, (TOKENS, HEADS), jnp.float32), -2.1, 2.1)
    offsets = jax.random.uniform(offset_key, (TOKENS // TOK_DEV, HEADS), jnp.float32, -0.7, 0.7)
    return jnp.repeat(offsets, TOK_DEV, axis=0) + jitter


def block_scale(own_key, extent, cuts, low, top_value):
    def one(dim, parts):
        draws = jax.random.uniform(jax.random.fold_in(jax.random.fold_in(own_key, 6), dim), (parts,), jnp.float32, low / len(cuts), top_value / len(cuts))
        return jnp.repeat(jnp.exp(draws), extent[dim] // parts).reshape((-1,) + (1,) * (len(extent) - dim - 1))

    factor_of = one(*cuts[0])
    for cut in cuts[1:]:
        factor_of = factor_of * one(*cut)
    return factor_of


def bell_draw(key, extent, width, reach, cuts=(), kind=jnp.bfloat16):
    drawn = width * jax.random.normal(key, extent, jnp.float32)
    if cuts:
        drawn = drawn * block_scale(key, extent, cuts, -0.22, 0.18)
    return jnp.clip(drawn, -reach, reach).astype(kind)


def setup_inputs(seed: int = 0, part: int = 0) -> dict:
    key_list = jax.random.split(jax.random.key(seed), 13)
    part_keys = jax.random.split(jax.random.fold_in(key_list[12], part), 13)
    x_in = bell_draw(part_keys[0], (TOKENS, HEADS * HEAD_DIM), 1.0, 6.0, ((0, 4), (1, 4)))
    bc_in = bell_draw(part_keys[1], (TOKENS, 2, GROUPS * STATE), 1.0, 6.0, ((0, 4), (2, 4)))
    z_in = bell_draw(part_keys[2], (TOKENS, HEADS * HEAD_DIM), 1.0, 6.0, ((0, 4), (1, 4)))
    dt_raw = draw_dt_raw(jax.random.fold_in(jax.random.fold_in(key_list[12], part), 71), part)
    conv_x = bell_draw(key_list[4], (KERNEL, HEADS * HEAD_DIM), KERNEL ** -0.5, 3.0, ((1, 4),))
    conv_bc = bell_draw(key_list[5], (KERNEL, 2, GROUPS * STATE), KERNEL ** -0.5, 3.0, ((2, 4),))
    conv_bias_x = jnp.clip(-0.9 + 0.79999997 * jax.random.uniform(key_list[6], (HEADS * HEAD_DIM,), jnp.float32) ** block_scale(key_list[6], (HEADS * HEAD_DIM,), ((0, 4),), -0.2, 0.2), -0.9, -0.1)
    conv_bias_bc = jnp.clip(-0.9 + 0.79999997 * jax.random.uniform(key_list[7], (2, GROUPS * STATE), jnp.float32) ** block_scale(key_list[7], (2, GROUPS * STATE), ((1, 4),), -0.2, 0.2), -0.9, -0.1)
    dt_bias = draw_dt_bias(jax.random.fold_in(key_list[12], 71), part)
    a_log = draw_a_log(jax.random.fold_in(key_list[12], 71), part)
    d_skip = jnp.clip(0.5 + 1.5 * jax.random.uniform(key_list[10], (HEADS,), jnp.float32) ** block_scale(key_list[10], (HEADS,), ((0, 4),), -0.2, 0.2), 0.5, 2.0)
    norm_gain = jnp.clip(1.0 + 0.1 * jax.random.normal(key_list[11], (HEADS * HEAD_DIM,), jnp.float32), 0.5, 1.5)
    return {"x_in": x_in, "bc_in": bc_in, "z_in": z_in, "dt_raw": dt_raw, "conv_x": conv_x, "conv_bc": conv_bc, "conv_bias_x": conv_bias_x, "conv_bias_bc": conv_bias_bc, "dt_bias": dt_bias, "a_log": a_log, "d_skip": d_skip, "norm_gain": norm_gain}


eps = 1e-05

def conv_valid(padded, weight, offset_bias):
    lag_rows = weight.shape[0] - 1
    length = padded.shape[0] - lag_rows
    total = jnp.zeros((length,) + padded.shape[1:], jnp.float32) + offset_bias.astype(jnp.float32)
    for position in range(weight.shape[0]):
        total = total + padded[position:position + length].astype(jnp.float32) * weight[position].astype(jnp.float32)
    return jax.nn.silu(total).astype(jnp.bfloat16)

def span_parts(x_span, b_span, step_span, log_span):
    cumul = jnp.cumsum(log_span, axis=0)
    tail_fade = jnp.exp(cumul[-1][None] - cumul) * step_span
    scaled = tail_fade[..., None] * x_span
    contrib = jnp.einsum('sghp,sgn->ghpn', scaled, b_span, precision=lax.Precision.HIGHEST)
    return (contrib, jnp.exp(cumul[-1]))

def span_output(carried, x_span, b_span, c_span, step_span, log_span):
    cumul = jnp.cumsum(log_span, axis=0)
    length = cumul.shape[0]
    scores = jnp.einsum('tgn,sgn->tsg', c_span, b_span, precision=lax.Precision.HIGHEST)
    places = jnp.arange(length)
    causal = places[:, None] >= places[None, :]
    spacing = cumul[:, None] - cumul[None, :]
    decay_mat = jnp.exp(jnp.where(causal[:, :, None, None], spacing, -jnp.inf))
    weights = decay_mat * scores[..., None] * step_span[None]
    inside = jnp.einsum('tsgh,sghp->tghp', weights, x_span, precision=lax.Precision.HIGHEST)
    readout = jnp.einsum('tgn,ghpn->tghp', c_span, carried, precision=lax.Precision.HIGHEST)
    return inside + jnp.exp(cumul)[..., None] * readout

def reference(x_in, bc_in, z_in, dt_raw, conv_x, conv_bc, conv_bias_x, conv_bias_bc, dt_bias, a_log, d_skip, norm_gain):
    lag_rows = KERNEL - 1
    x_conv = conv_valid(jnp.concatenate([jnp.zeros((lag_rows, x_in.shape[1]), x_in.dtype), x_in], 0), conv_x, conv_bias_x)
    bc_conv = conv_valid(jnp.concatenate([jnp.zeros((lag_rows,) + bc_in.shape[1:], bc_in.dtype), bc_in], 0), conv_bc, conv_bias_bc)
    per_group = HEADS // GROUPS
    x_heads = x_conv.astype(jnp.float32).reshape(TOKENS, GROUPS, per_group, HEAD_DIM)
    b_all = bc_conv[:, 0].astype(jnp.float32).reshape(TOKENS, GROUPS, STATE)
    c_all = bc_conv[:, 1].astype(jnp.float32).reshape(TOKENS, GROUPS, STATE)
    step_size = jax.nn.softplus(dt_raw + dt_bias[None]).reshape(TOKENS, GROUPS, per_group)
    log_fade = (-jnp.exp(a_log)).reshape(GROUPS, per_group)[None] * step_size
    blocks = TOKENS // SPAN

    def by_block(values):
        return values.reshape((blocks, SPAN) + values.shape[1:])
    inputs = (by_block(x_heads), by_block(b_all), by_block(c_all), by_block(step_size), by_block(log_fade))

    def advance(carried, pieces):
        output = span_output(carried, pieces[0], pieces[1], pieces[2], pieces[3], pieces[4])
        contrib, fading = span_parts(pieces[0], pieces[1], pieces[3], pieces[4])
        return (fading[..., None, None] * carried + contrib, output)
    zero_state = jnp.zeros((GROUPS, per_group, HEAD_DIM, STATE), jnp.float32)
    last_state, outputs = lax.scan(advance, zero_state, inputs)
    ssm_out = outputs.reshape(TOKENS, GROUPS, per_group, HEAD_DIM)
    ssm_out = ssm_out + d_skip.reshape(GROUPS, per_group)[None, :, :, None] * x_heads
    gate_vals = jax.nn.silu(z_in.astype(jnp.float32)).reshape(TOKENS, GROUPS, per_group * HEAD_DIM)
    gated = ssm_out.reshape(TOKENS, GROUPS, per_group * HEAD_DIM) * gate_vals
    meansq = lax.optimization_barrier(jnp.mean(gated * gated, axis=-1, keepdims=True))
    normed = gated * lax.rsqrt(meansq + eps) * norm_gain.reshape(GROUPS, per_group * HEAD_DIM)[None]
    mixed = normed.astype(jnp.bfloat16).reshape(TOKENS, HEADS * HEAD_DIM)
    final_state = last_state.reshape(HEADS, HEAD_DIM, STATE)
    return (mixed, final_state)
```

```python
import functools
import math

import jax
import jax.numpy as jnp
from jax import lax
from jax.experimental import pallas as pl
from jax.experimental.pallas import tpu as pltpu
from jax.sharding import PartitionSpec as P

HEAD_DIM = 64
STATE = 256
SPAN = 128
CHUNK = 512
HEADS_CHUNK = CHUNK // HEAD_DIM
HALO = 8
LOG2E = math.log2(math.e)

eps = 1e-05
F32 = jnp.float32
BF16 = jnp.bfloat16


def silu(v):
    half = 0.5 * v
    return half * jnp.tanh(half) + half


def dot(a, b):
    return jnp.dot(a, b, preferred_element_type=F32)


def params():
    return pltpu.CompilerParams(
        dimension_semantics=("arbitrary",), vmem_limit_bytes=48 << 20
    )


def local_kernel(x_ref, halo_ref, taps_ref, bias_ref, tail_ref, spread_ref, bt_ref, xc_ref, st_ref):
    rows = x_ref.shape[0]
    step = 64
    taps = taps_ref[...].astype(F32)
    bias = bias_ref[...]
    lag = taps.shape[0] - 1
    before = halo_ref[...].astype(F32)
    total = None
    for r in range(0, rows, step):
        here = x_ref[r : r + step].astype(F32)
        window = jnp.concatenate([before, here], axis=0)
        before = here[step - HALO :]
        acc = bias + here * taps[lag][None]
        for k in range(lag):
            at = HALO - lag + k
            acc = acc + window[at : at + step] * taps[k][None]
        conv = silu(acc).astype(BF16)
        xc_ref[r : r + step] = conv
    for r in range(0, rows, SPAN):
        weight = dot(tail_ref[r : r + SPAN], spread_ref[...])
        scaled = (xc_ref[r : r + SPAN].astype(F32) * weight).astype(BF16)
        part = dot(bt_ref[:, r : r + SPAN], scaled)
        total = part if total is None else total + part
    st_ref[...] = total.astype(BF16)


def local_states(x, halo, taps, bias, tail, spread, b_t):
    rows, channels = x.shape
    group = channels // (b_t.shape[0] // STATE)
    per = group // CHUNK
    heads = tail.shape[1]
    return pl.pallas_call(
        local_kernel,
        grid=(channels // CHUNK,),
        in_specs=[
            pl.BlockSpec((rows, CHUNK), lambda j: (0, j)),
            pl.BlockSpec((HALO, CHUNK), lambda j: (0, j)),
            pl.BlockSpec((taps.shape[0], CHUNK), lambda j: (0, j)),
            pl.BlockSpec((1, CHUNK), lambda j: (0, j)),
            pl.BlockSpec((rows, heads), lambda j: (0, 0)),
            pl.BlockSpec((heads, CHUNK), lambda j: (0, j)),
            pl.BlockSpec((STATE, rows), lambda j: (j // per, 0)),
        ],
        out_specs=[
            pl.BlockSpec((rows, CHUNK), lambda j: (0, j)),
            pl.BlockSpec((STATE, CHUNK), lambda j: (0, j)),
        ],
        out_shape=[
            jax.ShapeDtypeStruct((rows, channels), BF16),
            jax.ShapeDtypeStruct((STATE, channels), BF16),
        ],
        compiler_params=params(),
        cost_estimate=pl.CostEstimate(
            flops=2 * rows * channels * STATE, bytes_accessed=4 * rows * channels, transcendentals=rows * channels
        ),
    )(x, halo, taps, bias, tail, spread, b_t)


def inside_kernel(
    x_ref, c_ref, bt_ref, col_ref, row_ref, tail_ref, entry_ref, spread_ref, fade_ref, skip_ref, y_ref, st_ref
):
    rows = x_ref.shape[0]
    spans = rows // SPAN
    causal = lax.broadcasted_iota(jnp.int32, (SPAN, SPAN), 0) >= lax.broadcasted_iota(
        jnp.int32, (SPAN, SPAN), 1
    )
    low = lax.broadcasted_iota(jnp.int32, (SPAN, 2 * HEAD_DIM), 1) < HEAD_DIM
    none = jnp.zeros((), BF16)
    for k in range(spans):
        at = slice(k * SPAN, (k + 1) * SPAN)
        c_span = c_ref[at]
        scores = dot(c_span, bt_ref[:, at])
        x_span = x_ref[at]
        out = x_span.astype(F32) * skip_ref[...]
        if k > 0:
            entry = dot(entry_ref[at], spread_ref[...])
            out = out + entry * dot(c_span, st_ref[...].astype(BF16))
        y_ref[at] = out.astype(BF16)
        for pair in range(HEADS_CHUNK // 2):
            weights = []
            for h in (2 * pair, 2 * pair + 1):
                spacing = col_ref[0, at, h : h + 1] - row_ref[h : h + 1, at]
                decay = jnp.exp2(jnp.where(causal, spacing, -jnp.inf))
                weights.append((decay * scores).astype(BF16))
            lanes = slice(pair * 2 * HEAD_DIM, (pair + 1) * 2 * HEAD_DIM)
            x_pair = x_span[:, lanes]
            stacked = jnp.concatenate(
                [jnp.where(low, x_pair, none), jnp.where(low, none, x_pair)], axis=0
            )
            within = dot(jnp.concatenate(weights, axis=1), stacked)
            y_ref[at, lanes] = (out[:, lanes] + within).astype(BF16)
        if k < spans - 1:
            weight = dot(tail_ref[at], spread_ref[...])
            scaled = (x_span.astype(F32) * weight).astype(BF16)
            part = dot(bt_ref[:, at], scaled)
            if k > 0:
                part = part + fade_ref[k : k + 1] * st_ref[...]
            st_ref[...] = part


def inside(xc, c_all, b_t, col, row, tail, entry, spread, fade, skip):
    rows, channels = xc.shape
    group = channels // (b_t.shape[0] // STATE)
    per = group // CHUNK
    heads = tail.shape[1]
    return pl.pallas_call(
        inside_kernel,
        grid=(channels // CHUNK,),
        in_specs=[
            pl.BlockSpec((rows, CHUNK), lambda j: (0, j)),
            pl.BlockSpec((rows, STATE), lambda j: (0, j // per)),
            pl.BlockSpec((STATE, rows), lambda j: (j // per, 0)),
            pl.BlockSpec((1, rows, HEADS_CHUNK), lambda j: (j, 0, 0)),
            pl.BlockSpec((HEADS_CHUNK, rows), lambda j: (j, 0)),
            pl.BlockSpec((rows, heads), lambda j: (0, 0)),
            pl.BlockSpec((rows, heads), lambda j: (0, 0)),
            pl.BlockSpec((heads, CHUNK), lambda j: (0, j)),
            pl.BlockSpec((fade.shape[0], CHUNK), lambda j: (0, j)),
            pl.BlockSpec((1, CHUNK), lambda j: (0, j)),
        ],
        out_specs=pl.BlockSpec((rows, CHUNK), lambda j: (0, j)),
        out_shape=jax.ShapeDtypeStruct((rows, channels), BF16),
        scratch_shapes=[pltpu.VMEM((STATE, CHUNK), F32)],
        compiler_params=params(),
        cost_estimate=pl.CostEstimate(
            flops=20 * rows * channels * STATE, bytes_accessed=4 * rows * channels, transcendentals=4 * rows * channels
        ),
    )(xc, c_all, b_t, col, row, tail, entry, spread, fade, skip)


def finish_kernel(y_ref, z_ref, c_ref, state_ref, entry_ref, spread_ref, gain_ref, out_ref):
    entry = dot(entry_ref[...], spread_ref[...])
    y = y_ref[...].astype(F32) + entry * dot(c_ref[...], state_ref[...])
    gated = y * silu(z_ref[...].astype(F32))
    meansq = jnp.mean(gated * gated, axis=-1, keepdims=True)
    out_ref[...] = (gated * lax.rsqrt(meansq + eps) * gain_ref[...]).astype(BF16)


def finish(y, z, c_all, state_in, entry, spread, gain):
    rows, channels = y.shape
    groups = c_all.shape[1] // STATE
    width = channels // groups
    heads = entry.shape[1]
    blocks = rows // SPAN
    return pl.pallas_call(
        finish_kernel,
        grid=(groups * blocks,),
        in_specs=[
            pl.BlockSpec((SPAN, width), lambda j: (j % blocks, j // blocks)),
            pl.BlockSpec((SPAN, width), lambda j: (j % blocks, j // blocks)),
            pl.BlockSpec((SPAN, STATE), lambda j: (j % blocks, j // blocks)),
            pl.BlockSpec((STATE, width), lambda j: (0, j // blocks)),
            pl.BlockSpec((SPAN, heads), lambda j: (j % blocks, 0)),
            pl.BlockSpec((heads, width), lambda j: (0, j // blocks)),
            pl.BlockSpec((1, width), lambda j: (0, j // blocks)),
        ],
        out_specs=pl.BlockSpec((SPAN, width), lambda j: (j % blocks, j // blocks)),
        out_shape=jax.ShapeDtypeStruct((rows, channels), BF16),
        compiler_params=params(),
        cost_estimate=pl.CostEstimate(
            flops=2 * rows * channels * STATE, bytes_accessed=6 * rows * channels, transcendentals=rows * channels
        ),
    )(y, z, c_all, state_in, entry, spread, gain)


def passed_along(block, axis, distance):
    devices = range(lax.axis_size(axis))
    route = [(i - distance, i) for i in devices if i - distance in devices]
    return lax.ppermute(block, axis, route)


def conv_valid(padded, weight, offset_bias):
    lag_rows = weight.shape[0] - 1
    length = padded.shape[0] - lag_rows
    total = jnp.zeros((length,) + padded.shape[1:], F32) + offset_bias
    for position in range(weight.shape[0]):
        total = total + padded[position : position + length].astype(F32) * weight[position].astype(F32)
    return jax.nn.silu(total).astype(BF16)


def per_device(
    x_in,
    bc_in,
    z_in,
    dt_raw,
    conv_x,
    conv_bc,
    conv_bias_x,
    conv_bias_bc,
    dt_bias,
    a_log,
    d_skip,
    norm_gain,
):
    rows, channels = x_in.shape
    heads = dt_raw.shape[1]
    groups = bc_in.shape[2] // STATE
    lag = conv_x.shape[0] - 1
    spans = rows // SPAN
    n = lax.axis_size("ctx")
    me = lax.axis_index("ctx")
    earlier = passed_along((x_in[rows - lag :], bc_in[rows - lag :]), "ctx", 1)
    halo = jnp.pad(earlier[0], ((HALO - lag, 0), (0, 0)))
    bc_conv = conv_valid(jnp.concatenate([earlier[1], bc_in], 0), conv_bc, conv_bias_bc)
    b_t = bc_conv[:, 0].T
    c_all = bc_conv[:, 1]

    step = jax.nn.softplus(dt_raw + dt_bias[None])
    fade = (-LOG2E * jnp.exp(a_log))[None] * step
    lower = jnp.tril(jnp.ones((SPAN, SPAN), F32))
    cumul = jnp.einsum(
        "ts,ksh->kth", lower, fade.reshape(spans, SPAN, heads), precision=lax.Precision.HIGHEST
    )
    last = cumul[:, -1]
    upto = jnp.cumsum(last, axis=0)
    total = upto[-1]
    cumul_dev = cumul + (upto - last)[:, None]
    cumul = cumul.reshape(rows, heads)
    cumul_dev_flat = cumul_dev.reshape(rows, heads)
    tail_dev = (jnp.exp2(total[None] - cumul_dev_flat) * step).astype(BF16)
    tail = (
        jnp.exp2(last[:, None] - cumul.reshape(spans, SPAN, heads)).reshape(rows, heads) * step
    ).astype(BF16)
    entry = jnp.exp2(cumul).astype(BF16)
    entry_dev = jnp.exp2(cumul_dev_flat).astype(BF16)
    col = cumul.reshape(rows, heads // HEADS_CHUNK, HEADS_CHUNK).transpose(1, 0, 2)
    row = (cumul - jnp.log2(step)).T
    span_fade = jnp.repeat(jnp.exp2(last), HEAD_DIM, axis=1)
    whole_fade = jnp.repeat(jnp.exp2(total), HEAD_DIM)[None]
    spread = (
        lax.broadcasted_iota(jnp.int32, (heads, channels), 1) // HEAD_DIM
        == lax.broadcasted_iota(jnp.int32, (heads, channels), 0)
    ).astype(BF16)
    skip = jnp.repeat(d_skip, HEAD_DIM)[None]

    xc, local = local_states(x_in, halo, conv_x, conv_bias_x[None], tail_dev, spread, b_t)

    width = channels // groups
    ins, outs = [], []
    for g in range(groups):
        part = slice(g * width, (g + 1) * width)
        mine = local[:, part].astype(F32)
        current = local[:, part]
        state_in = jnp.zeros_like(current)
        for hop in range(n - 1):
            got = lax.ppermute(current, "ctx", [(hop, hop + 1)])
            arrived = me == hop + 1
            state_in = jnp.where(arrived, got, state_in)
            joined = (whole_fade[:, part] * got.astype(F32) + mine).astype(BF16)
            current = jnp.where(arrived, joined, current)
        ins.append(state_in)
        outs.append(current)
    state_in = jnp.concatenate(ins, axis=1)
    final = jnp.concatenate(outs, axis=1)
    y = inside(xc, c_all, b_t, col, row, tail, entry, spread, span_fade, skip)
    mixed = finish(y, z_in, c_all, state_in, entry_dev, spread, norm_gain[None])

    share = STATE // n
    piece = final[(n - 1) * share :]
    for j in range(n - 1):
        got = lax.ppermute(final[j * share : (j + 1) * share], "ctx", [(n - 1, j)])
        piece = jnp.where(me == j, got, piece)
    final_share = piece.astype(F32).reshape(share, heads, HEAD_DIM).transpose(1, 2, 0)
    return (mixed, final_share)


def solution(mesh):
    in_specs = (
        P(("group", "ctx"), "tp"),
        P(("group", "ctx"), None, "tp"),
        P(("group", "ctx"), "tp"),
        P(("group", "ctx"), "tp"),
        P(None, "tp"),
        P(None, None, "tp"),
        P("tp"),
        P(None, "tp"),
        P("tp"),
        P("tp"),
        P("tp"),
        P("tp"),
    )
    out_specs = (P(("group", "ctx"), "tp"), P(("group", "tp"), None, "ctx"))
    return jax.shard_map(
        per_device, mesh=mesh, in_specs=in_specs, out_specs=out_specs, check_vma=False
    )
```

```python
import functools
import math

import jax
import jax.numpy as jnp
from jax import lax
from jax.experimental import pallas as pl
from jax.experimental.pallas import tpu as pltpu
from jax.sharding import PartitionSpec as P

HEAD_DIM = 64
STATE = 256
SPAN = 128
CHUNK = 512
HEADS_CHUNK = CHUNK // HEAD_DIM
HALO = 8
LOG2E = math.log2(math.e)

eps = 1e-05
F32 = jnp.float32
BF16 = jnp.bfloat16


def silu(v):
    half = 0.5 * v
    return half * jnp.tanh(half) + half


def dot(a, b):
    return jnp.dot(a, b, preferred_element_type=F32)


def params():
    return pltpu.CompilerParams(
        dimension_semantics=("arbitrary",), vmem_limit_bytes=48 << 20
    )


def finish_kernel(y_ref, z_ref, c_ref, state_ref, entry_ref, spread_ref, gain_ref, out_ref):
    entry = dot(entry_ref[...], spread_ref[...])
    y = y_ref[...].astype(F32) + entry * dot(c_ref[...], state_ref[...])
    gated = y * silu(z_ref[...].astype(F32))
    meansq = jnp.mean(gated * gated, axis=-1, keepdims=True)
    out_ref[...] = (gated * lax.rsqrt(meansq + eps) * gain_ref[...]).astype(BF16)


def finish(y, z, c_all, state_in, entry, spread, gain):
    rows, channels = y.shape
    groups = c_all.shape[1] // STATE
    width = channels // groups
    heads = entry.shape[1]
    blocks = rows // SPAN
    return pl.pallas_call(
        finish_kernel,
        grid=(groups * blocks,),
        in_specs=[
            pl.BlockSpec((SPAN, width), lambda j: (j % blocks, j // blocks)),
            pl.BlockSpec((SPAN, width), lambda j: (j % blocks, j // blocks)),
            pl.BlockSpec((SPAN, STATE), lambda j: (j % blocks, j // blocks)),
            pl.BlockSpec((STATE, width), lambda j: (0, j // blocks)),
            pl.BlockSpec((SPAN, heads), lambda j: (j % blocks, 0)),
            pl.BlockSpec((heads, width), lambda j: (0, j // blocks)),
            pl.BlockSpec((1, width), lambda j: (0, j // blocks)),
        ],
        out_specs=pl.BlockSpec((SPAN, width), lambda j: (j % blocks, j // blocks)),
        out_shape=jax.ShapeDtypeStruct((rows, channels), BF16),
        compiler_params=params(),
        cost_estimate=pl.CostEstimate(
            flops=2 * rows * channels * STATE, bytes_accessed=6 * rows * channels, transcendentals=rows * channels
        ),
    )(y, z, c_all, state_in, entry, spread, gain)


EDGE = 16
MESH = pl.DeviceIdType.MESH


def conv_rows(read, before, taps, bias, rows, write):
    step = 64
    lag = taps.shape[0] - 1
    for r in range(0, rows, step):
        here = read(r, step).astype(F32)
        window = jnp.concatenate([before, here], axis=0)
        before = here[step - HALO :]
        acc = bias + here * taps[lag][None]
        for k in range(lag):
            at = HALO - lag + k
            acc = acc + window[at : at + step] * taps[k][None]
        write(r, step, silu(acc))


def exact_dot(a, b):
    return jnp.dot(a, b, preferred_element_type=F32, precision=lax.Precision.HIGHEST)


def scan_kernel(
    n,
    x_ref,
    taps_ref,
    bias_ref,
    bc_ref,
    taps_bc_ref,
    bias_bc_ref,
    dt_ref,
    dt_bias_ref,
    a_log_ref,
    skip_ref,
    x_any,
    bc_any,
    y_ref,
    c_out,
    state_out,
    entry_out,
    final_out,
    xc,
    sent,
    came,
    piece,
    st_ref,
    col_ref,
    row_ref,
    tail_dev_ref,
    tail_ref,
    entry_ref,
    fade_ref,
    bt_ref,
    c_ref,
    edge_x,
    edge_bc,
    send_sem,
    recv_sem,
    piece_send,
    piece_recv,
    edge_send,
    edge_recv,
):
    s = pl.program_id(0)
    chunks = sent.shape[0]
    last_step = 2 * chunks - 1
    me = lax.axis_index("ctx")
    rows = x_ref.shape[0]
    spans = rows // SPAN
    heads = dt_ref.shape[1]
    groups = bt_ref.shape[0]
    per = chunks // groups
    share = STATE // n
    right = jnp.minimum(me + 1, n - 1)
    phase = s // chunks
    j = s % chunks

    def edge_copies():
        return [
            pltpu.make_async_remote_copy(
                src_ref=whole.at[pl.ds(rows - EDGE, EDGE)],
                dst_ref=edge,
                send_sem=edge_send.at[i],
                recv_sem=edge_recv.at[i],
                device_id={"ctx": right},
                device_id_type=MESH,
            )
            for i, (whole, edge) in enumerate(((bc_any, edge_bc), (x_any, edge_x)))
        ]

    def onward(c):
        return pltpu.make_async_remote_copy(
            src_ref=sent.at[c],
            dst_ref=came.at[c],
            send_sem=send_sem.at[c],
            recv_sem=recv_sem.at[c],
            device_id={"ctx": right},
            device_id_type=MESH,
        )

    def handed(q, c):
        return pltpu.make_async_remote_copy(
            src_ref=sent.at[c, pl.ds(pl.multiple_of(q * share, share), share)],
            dst_ref=piece.at[c],
            send_sem=piece_send.at[q, c],
            recv_sem=piece_recv.at[c],
            device_id={"ctx": q},
            device_id_type=MESH,
        )

    def spread_of(c):
        shape = (heads, CHUNK)
        return (
            lax.broadcasted_iota(jnp.int32, shape, 1) // HEAD_DIM + c * HEADS_CHUNK
            == lax.broadcasted_iota(jnp.int32, shape, 0)
        ).astype(F32)

    @pl.when(s == 0)
    def _():
        barrier = pltpu.get_barrier_semaphore()
        for k in range(1, n):
            pl.semaphore_signal(
                barrier, inc=1, device_id={"ctx": lax.rem(me + k, n)}, device_id_type=MESH
            )
        pl.semaphore_wait(barrier, n - 1)

        @pl.when(me < n - 1)
        def _():
            for copy in edge_copies():
                copy.start()

        rate = -LOG2E * jnp.exp(a_log_ref[...])
        lower = (
            lax.broadcasted_iota(jnp.int32, (SPAN, SPAN), 0)
            >= lax.broadcasted_iota(jnp.int32, (SPAN, SPAN), 1)
        ).astype(F32)
        steps, sums = [], []
        so_far = jnp.zeros((1, heads), F32)
        starts = []
        for k in range(spans):
            at = slice(k * SPAN, (k + 1) * SPAN)
            v = dt_ref[at] + dt_bias_ref[...]
            step = jnp.maximum(v, 0.0) + jnp.log1p(jnp.exp(-jnp.abs(v)))
            cumul = exact_dot(lower, step * rate)
            last = cumul[SPAN - 1 :]
            tail_ref[at] = (jnp.exp2(last - cumul) * step).astype(BF16)
            entry_ref[at] = jnp.exp2(cumul).astype(BF16)
            entry_out[at] = jnp.exp2(cumul + so_far).astype(BF16)
            fade_ref[k : k + 1] = jnp.exp2(last)
            steps.append(step)
            sums.append(cumul)
            starts.append(so_far)
            so_far = so_far + last
        fade_ref[spans : spans + 1] = jnp.exp2(so_far)
        fade_ref[spans + 1 : spans + 2] = skip_ref[...]
        fade_ref[spans + 2 :] = jnp.zeros((fade_ref.shape[0] - spans - 2, heads), F32)
        for k in range(spans):
            at = slice(k * SPAN, (k + 1) * SPAN)
            tail_dev_ref[at] = (jnp.exp2(so_far - (sums[k] + starts[k])) * steps[k]).astype(BF16)
            for c in range(chunks):
                col_ref[c, at] = sums[k][:, c * HEADS_CHUNK : (c + 1) * HEADS_CHUNK]
            rowed = sums[k] - jnp.log2(steps[k])
            wide = jnp.concatenate([rowed] * (128 // heads), axis=1) if heads < 128 else rowed
            row_ref[:, at] = wide.T[:heads]

        @pl.when(me == 0)
        def _():
            edge_x[...] = jnp.zeros_like(edge_x)
            edge_bc[...] = jnp.zeros_like(edge_bc)
            state_out[...] = jnp.zeros_like(state_out)

        @pl.when(me > 0)
        def _():
            for copy in edge_copies():
                copy.wait_recv()

        for side in range(2):
            for g in range(groups):
                lanes = slice((side * groups + g) * STATE, (side * groups + g + 1) * STATE)

                def write(r, size, value, g=g, side=side):
                    if side == 0:
                        bt_ref[g, :, r : r + size] = value.astype(BF16).astype(F32).T.astype(BF16)
                    else:
                        c_ref[g, r : r + size] = value.astype(BF16)
                        c_out[r : r + size, g * STATE : (g + 1) * STATE] = value.astype(BF16)

                rows_at = SPAN
                lag = taps_bc_ref.shape[0] - 1
                before = edge_bc[:, lanes].astype(F32)[EDGE - HALO :]
                taps = taps_bc_ref[:, lanes].astype(F32)
                for r in range(0, rows, rows_at):
                    here = bc_ref[r : r + rows_at, lanes].astype(F32)
                    window = jnp.concatenate([before, here], axis=0)
                    before = here[rows_at - HALO :]
                    acc = bias_bc_ref[:, lanes] + here * taps[lag][None]
                    for k in range(lag):
                        first = HALO - lag + k
                        acc = acc + window[first : first + rows_at] * taps[k][None]
                    write(r, rows_at, silu(acc))

    def join(c, carry):
        onward(c).wait_recv()
        got = came[c]
        state_out[:, pl.ds(pl.multiple_of(c * CHUNK, CHUNK), CHUNK)] = got
        fades = exact_dot(fade_ref[...], spread_of(c))
        mine = sent[c].astype(F32)
        sent[c] = (fades[spans : spans + 1] * got.astype(F32) + mine).astype(BF16)

        @pl.when(me < n - 1)
        def _():
            onward(c).start()

        @pl.when(me == n - 1)
        def _():
            lax.fori_loop(0, n - 1, lambda q, z: (handed(q, c).start(), z)[1], 0)

        return carry

    base = jnp.where(me == 1, 2, chunks - 3 + me)
    first = jnp.clip(s - base, 0, chunks)
    stop = jnp.where(s == last_step, chunks, jnp.clip(s - base + 1, 0, chunks))
    stop = jnp.where(me == 0, first, stop)
    lax.fori_loop(first, stop, join, 0)

    @pl.when(phase == 0)
    def _():
        spread = spread_of(j).astype(BF16)
        bt = bt_ref.at[j // per]
        taps = taps_ref[...].astype(F32)
        before = edge_x[:, pl.ds(pl.multiple_of(j * CHUNK, CHUNK), CHUNK)].astype(F32)[EDGE - HALO :]

        def write(r, size, value):
            xc[j, r : r + size] = value.astype(BF16)

        conv_rows(lambda r, size: x_ref[r : r + size], before, taps, bias_ref[...], rows, write)
        total = None
        for r in range(0, rows, SPAN):
            weight = dot(tail_dev_ref[r : r + SPAN], spread)
            scaled = (xc[j, r : r + SPAN].astype(F32) * weight).astype(BF16)
            part = dot(bt[:, r : r + SPAN], scaled)
            total = part if total is None else total + part
        sent[j] = total.astype(BF16)

        @pl.when(me == 0)
        def _():
            onward(j).start()

    @pl.when(phase == 1)
    def _():
        spread = spread_of(j)
        fades = exact_dot(fade_ref[...], spread)
        spread = spread.astype(BF16)
        g = j // per
        causal = lax.broadcasted_iota(jnp.int32, (SPAN, SPAN), 0) >= lax.broadcasted_iota(
            jnp.int32, (SPAN, SPAN), 1
        )
        low = lax.broadcasted_iota(jnp.int32, (SPAN, 2 * HEAD_DIM), 1) < HEAD_DIM
        none = jnp.zeros((), BF16)
        head_rows = pl.ds(pl.multiple_of(j * HEADS_CHUNK, HEADS_CHUNK), HEADS_CHUNK)
        for k in range(spans):
            at = slice(k * SPAN, (k + 1) * SPAN)
            c_span = c_ref[g, at]
            b_span = bt_ref[g, :, at]
            scores = dot(c_span, b_span)
            x_span = xc[j, at]
            row_span = row_ref[head_rows, at]
            out = x_span.astype(F32) * fades[spans + 1 : spans + 2]
            if k > 0:
                entry = dot(entry_ref[at], spread)
                out = out + entry * dot(c_span, st_ref[...].astype(BF16))
            for pair in range(HEADS_CHUNK // 2):
                weights = []
                for h in (2 * pair, 2 * pair + 1):
                    spacing = col_ref[j, at, h : h + 1] - row_span[h : h + 1]
                    decay = jnp.exp2(jnp.where(causal, spacing, -jnp.inf))
                    weights.append((decay * scores).astype(BF16))
                lanes = slice(pair * 2 * HEAD_DIM, (pair + 1) * 2 * HEAD_DIM)
                x_pair = x_span[:, lanes]
                stacked = jnp.concatenate(
                    [jnp.where(low, x_pair, none), jnp.where(low, none, x_pair)], axis=0
                )
                within = dot(jnp.concatenate(weights, axis=1), stacked)
                y_ref[at, lanes] = (out[:, lanes] + within).astype(BF16)
            if k < spans - 1:
                weight = dot(tail_ref[at], spread)
                scaled = (x_span.astype(F32) * weight).astype(BF16)
                part = dot(b_span, scaled)
                if k > 0:
                    part = part + fades[k : k + 1] * st_ref[...]
                st_ref[...] = part

    @pl.when(s == last_step)
    def _():
        @pl.when(me < n - 1)
        def _():
            for copy in edge_copies():
                copy.wait_send()
            for c in range(chunks):
                onward(c).wait_send()
            for c in range(chunks):
                handed(0, c).wait_recv()
                final_out[:, c * CHUNK : (c + 1) * CHUNK] = piece[c]

        @pl.when(me == n - 1)
        def _():
            for c in range(chunks):
                lax.fori_loop(0, n - 1, lambda q, z: (handed(q, c).wait_send(), z)[1], 0)
                final_out[:, c * CHUNK : (c + 1) * CHUNK] = sent[c, (n - 1) * share :]


def scan(n, x, taps, bias, bc, taps_bc, bias_bc, dt, dt_bias, a_log, skip):
    rows, channels = x.shape
    chunks = channels // CHUNK
    heads = dt.shape[1]
    width = bc.shape[1]
    groups = width // (2 * STATE)
    share = STATE // n
    spans = rows // SPAN
    turn = lambda s: (0, jnp.minimum(s, chunks - 1))
    still = lambda s: (0, 0)
    return pl.pallas_call(
        functools.partial(scan_kernel, n),
        grid=(2 * chunks,),
        in_specs=[
            pl.BlockSpec((rows, CHUNK), turn),
            pl.BlockSpec((taps.shape[0], CHUNK), turn),
            pl.BlockSpec((1, CHUNK), turn),
            pl.BlockSpec((rows, width), still),
            pl.BlockSpec((taps.shape[0], width), still),
            pl.BlockSpec((1, width), still),
            pl.BlockSpec((rows, heads), still),
            pl.BlockSpec((1, heads), still),
            pl.BlockSpec((1, heads), still),
            pl.BlockSpec((1, heads), still),
            pl.BlockSpec(memory_space=pl.ANY),
            pl.BlockSpec(memory_space=pl.ANY),
        ],
        out_specs=[
            pl.BlockSpec((rows, CHUNK), lambda s: (0, jnp.maximum(s - chunks, 0))),
            pl.BlockSpec((rows, groups * STATE), still),
            pl.BlockSpec((STATE, channels), still),
            pl.BlockSpec((rows, heads), still),
            pl.BlockSpec((share, channels), still),
        ],
        out_shape=[
            jax.ShapeDtypeStruct((rows, channels), BF16),
            jax.ShapeDtypeStruct((rows, groups * STATE), BF16),
            jax.ShapeDtypeStruct((STATE, channels), BF16),
            jax.ShapeDtypeStruct((rows, heads), BF16),
            jax.ShapeDtypeStruct((share, channels), BF16),
        ],
        scratch_shapes=[
            pltpu.VMEM((chunks, rows, CHUNK), BF16),
            pltpu.VMEM((chunks, STATE, CHUNK), BF16),
            pltpu.VMEM((chunks, STATE, CHUNK), BF16),
            pltpu.VMEM((chunks, share, CHUNK), BF16),
            pltpu.VMEM((STATE, CHUNK), F32),
            pltpu.VMEM((chunks, rows, HEADS_CHUNK), F32),
            pltpu.VMEM((heads, rows), F32),
            pltpu.VMEM((rows, heads), BF16),
            pltpu.VMEM((rows, heads), BF16),
            pltpu.VMEM((rows, heads), BF16),
            pltpu.VMEM((-(-(spans + 2) // 8) * 8, heads), F32),
            pltpu.VMEM((groups, STATE, rows), BF16),
            pltpu.VMEM((groups, rows, STATE), BF16),
            pltpu.VMEM((EDGE, channels), BF16),
            pltpu.VMEM((EDGE, width), BF16),
            pltpu.SemaphoreType.DMA((chunks,)),
            pltpu.SemaphoreType.DMA((chunks,)),
            pltpu.SemaphoreType.DMA((n - 1, chunks)),
            pltpu.SemaphoreType.DMA((chunks,)),
            pltpu.SemaphoreType.DMA((2,)),
            pltpu.SemaphoreType.DMA((2,)),
        ],
        compiler_params=pltpu.CompilerParams(
            dimension_semantics=("arbitrary",),
            vmem_limit_bytes=56 << 20,
            collective_id=0,
            has_side_effects=True,
        ),
        cost_estimate=pl.CostEstimate(
            flops=20 * rows * channels * STATE, bytes_accessed=4 * rows * channels, transcendentals=4 * rows * channels
        ),
    )(x, taps, bias, bc, taps_bc, bias_bc, dt, dt_bias, a_log, skip, x, bc)


def per_device(
    x_in,
    bc_in,
    z_in,
    dt_raw,
    conv_x,
    conv_bc,
    conv_bias_x,
    conv_bias_bc,
    dt_bias,
    a_log,
    d_skip,
    norm_gain,
):
    rows, channels = x_in.shape
    heads = dt_raw.shape[1]
    n = lax.axis_size("ctx")
    width = 2 * bc_in.shape[2]
    y, c_all, state_in, entry, final = scan(
        n,
        x_in,
        conv_x,
        conv_bias_x[None],
        bc_in.reshape(rows, width),
        conv_bc.reshape(conv_bc.shape[0], width),
        conv_bias_bc.reshape(1, width),
        dt_raw,
        dt_bias[None],
        a_log[None],
        d_skip[None],
    )
    spread = (
        lax.broadcasted_iota(jnp.int32, (heads, channels), 1) // HEAD_DIM
        == lax.broadcasted_iota(jnp.int32, (heads, channels), 0)
    ).astype(BF16)
    mixed = finish(y, z_in, c_all, state_in, entry, spread, norm_gain[None])
    share = STATE // n
    final_share = final.astype(F32).reshape(share, heads, HEAD_DIM).transpose(1, 2, 0)
    return (mixed, final_share)


def solution(mesh):
    in_specs = (
        P(("group", "ctx"), "tp"),
        P(("group", "ctx"), None, "tp"),
        P(("group", "ctx"), "tp"),
        P(("group", "ctx"), "tp"),
        P(None, "tp"),
        P(None, None, "tp"),
        P("tp"),
        P(None, "tp"),
        P("tp"),
        P("tp"),
        P("tp"),
        P("tp"),
    )
    out_specs = (P(("group", "ctx"), "tp"), P(("group", "tp"), None, "ctx"))
    return jax.shard_map(
        per_device, mesh=mesh, in_specs=in_specs, out_specs=out_specs, check_vma=False
    )
```

```python
import functools
import math

import jax
import jax.numpy as jnp
from jax import lax
from jax.experimental import pallas as pl
from jax.experimental.pallas import tpu as pltpu
from jax.sharding import PartitionSpec as P

HEAD_DIM = 64
STATE = 256
SPAN = 128
CHUNK = 512
HEADS_CHUNK = CHUNK // HEAD_DIM
HALO = 8
LOG2E = math.log2(math.e)

eps = 1e-05
F32 = jnp.float32
BF16 = jnp.bfloat16


def silu(v):
    half = 0.5 * v
    return half * jnp.tanh(half) + half


def dot(a, b):
    return jnp.dot(a, b, preferred_element_type=F32)


def params():
    return pltpu.CompilerParams(
        dimension_semantics=("arbitrary",), vmem_limit_bytes=48 << 20
    )


def norm_kernel(gated_ref, gain_ref, out_ref):
    gated = gated_ref[...].astype(F32)
    meansq = jnp.mean(gated * gated, axis=-1, keepdims=True)
    out_ref[...] = (gated * lax.rsqrt(meansq + eps) * gain_ref[...]).astype(BF16)


def normed(gated, gain, groups):
    rows, channels = gated.shape
    width = channels // groups
    size = 2 * SPAN
    blocks = rows // size
    block = pl.BlockSpec((size, width), lambda j: (j % blocks, j // blocks))
    return pl.pallas_call(
        norm_kernel,
        grid=(groups * blocks,),
        in_specs=[block, pl.BlockSpec((1, width), lambda j: (0, j // blocks))],
        out_specs=block,
        out_shape=jax.ShapeDtypeStruct((rows, channels), BF16),
        compiler_params=params(),
        cost_estimate=pl.CostEstimate(
            flops=4 * rows * channels, bytes_accessed=4 * rows * channels, transcendentals=rows
        ),
    )(gated, gain)


EDGE = 16
MESH = pl.DeviceIdType.MESH


def conv_rows(read, before, taps, bias, rows, write):
    step = 64
    lag = taps.shape[0] - 1
    for r in range(0, rows, step):
        here = read(r, step).astype(F32)
        window = jnp.concatenate([before, here], axis=0)
        before = here[step - HALO :]
        acc = bias + here * taps[lag][None]
        for k in range(lag):
            at = HALO - lag + k
            acc = acc + window[at : at + step] * taps[k][None]
        write(r, step, silu(acc))


def leading(n, chunks):
    return chunks + max(0, n - 4)


def exact_dot(a, b):
    return jnp.dot(a, b, preferred_element_type=F32, precision=lax.Precision.HIGHEST)


def scan_kernel(
    n,
    x_ref,
    taps_ref,
    bias_ref,
    bc_ref,
    taps_bc_ref,
    bias_bc_ref,
    dt_ref,
    dt_bias_ref,
    a_log_ref,
    skip_ref,
    z_ref,
    x_any,
    bc_any,
    y_ref,
    final_out,
    xc,
    sent,
    came,
    piece,
    local,
    col_ref,
    row_ref,
    tail_ref,
    entry_ref,
    fade_ref,
    bt_ref,
    c_ref,
    edge_x,
    edge_bc,
    send_sem,
    recv_sem,
    piece_send,
    piece_recv,
    edge_send,
    edge_recv,
):
    s = pl.program_id(0)
    chunks = sent.shape[0]
    lead = leading(n, chunks)
    last_step = lead + chunks - 1
    me = lax.axis_index("ctx")
    rows = x_ref.shape[0]
    spans = rows // SPAN
    heads = dt_ref.shape[0]
    groups = bt_ref.shape[0]
    per = chunks // groups
    share = STATE // n
    right = jnp.minimum(me + 1, n - 1)

    def edge_copies():
        return [
            pltpu.make_async_remote_copy(
                src_ref=whole.at[pl.ds(rows - EDGE, EDGE)],
                dst_ref=edge,
                send_sem=edge_send.at[i],
                recv_sem=edge_recv.at[i],
                device_id={"ctx": right},
                device_id_type=MESH,
            )
            for i, (whole, edge) in enumerate(((bc_any, edge_bc), (x_any, edge_x)))
        ]

    def onward(c):
        return pltpu.make_async_remote_copy(
            src_ref=sent.at[c],
            dst_ref=came.at[c],
            send_sem=send_sem.at[c],
            recv_sem=recv_sem.at[c],
            device_id={"ctx": right},
            device_id_type=MESH,
        )

    def handed(q, c):
        return pltpu.make_async_remote_copy(
            src_ref=sent.at[c, pl.ds(pl.multiple_of(q * share, share), share)],
            dst_ref=piece.at[c],
            send_sem=piece_send.at[q, c],
            recv_sem=piece_recv.at[c],
            device_id={"ctx": q},
            device_id_type=MESH,
        )

    def spread_of(c):
        shape = (heads, CHUNK)
        return (
            lax.broadcasted_iota(jnp.int32, shape, 1) // HEAD_DIM + c * HEADS_CHUNK
            == lax.broadcasted_iota(jnp.int32, shape, 0)
        ).astype(F32)

    @pl.when(s == 0)
    def _():
        barrier = pltpu.get_barrier_semaphore()
        for k in range(1, n):
            pl.semaphore_signal(
                barrier, inc=1, device_id={"ctx": lax.rem(me + k, n)}, device_id_type=MESH
            )
        pl.semaphore_wait(barrier, n - 1)

        @pl.when(me < n - 1)
        def _():
            for copy in edge_copies():
                copy.start()

        rate = -LOG2E * jnp.exp(a_log_ref[...])
        lower = (
            lax.broadcasted_iota(jnp.int32, (SPAN, SPAN), 0)
            >= lax.broadcasted_iota(jnp.int32, (SPAN, SPAN), 1)
        ).astype(F32)
        so_far = jnp.zeros((1, heads), F32)
        for k in range(spans):
            at = slice(k * SPAN, (k + 1) * SPAN)
            v = dt_ref[:, at].T + dt_bias_ref[...]
            step = jnp.maximum(v, 0.0) + jnp.log1p(jnp.exp(-jnp.abs(v)))
            cumul = exact_dot(lower, step * rate)
            last = cumul[SPAN - 1 :]
            tail = jnp.exp2(last - cumul) * step
            entry = jnp.exp2(cumul)
            for c in range(chunks):
                mine = slice(c * HEADS_CHUNK, (c + 1) * HEADS_CHUNK)
                col_ref[c, at] = cumul[:, mine]
                tail_ref[c, at] = tail[:, mine]
                entry_ref[c, at] = entry[:, mine]
            rowed = cumul - jnp.log2(step)
            wide = jnp.concatenate([rowed] * (128 // heads), axis=1) if heads < 128 else rowed
            row_ref[:, at] = wide.T[:heads]
            fade_ref[k : k + 1] = jnp.exp2(last)
            fade_ref[spans + 2 + k : spans + 3 + k] = jnp.exp2(so_far)
            so_far = so_far + last
        fade_ref[spans : spans + 1] = jnp.exp2(so_far)
        fade_ref[spans + 1 : spans + 2] = skip_ref[...]
        if fade_ref.shape[0] > 2 * spans + 2:
            fade_ref[2 * spans + 2 :] = jnp.zeros((fade_ref.shape[0] - 2 * spans - 2, heads), F32)

        @pl.when(me == 0)
        def _():
            edge_x[...] = jnp.zeros_like(edge_x)
            edge_bc[...] = jnp.zeros_like(edge_bc)
            came[...] = jnp.zeros_like(came)

        @pl.when(me > 0)
        def _():
            for copy in edge_copies():
                copy.wait_recv()

        for side in range(2):
            for g in range(groups):
                lanes = slice((side * groups + g) * STATE, (side * groups + g + 1) * STATE)
                own = slice(g * STATE, (g + 1) * STATE)

                def write(r, size, value, g=g, side=side):
                    if side == 0:
                        bt_ref[g, :, r : r + size] = value.astype(BF16).astype(F32).T.astype(BF16)
                    else:
                        c_ref[g, r : r + size] = value.astype(BF16)

                rows_at = SPAN
                lag = taps_bc_ref.shape[0] - 1
                before = edge_bc[:, lanes].astype(F32)[EDGE - HALO :]
                taps = taps_bc_ref[:, side, own].astype(F32)
                for r in range(0, rows, rows_at):
                    here = bc_ref[r : r + rows_at, lanes].astype(F32)
                    window = jnp.concatenate([before, here], axis=0)
                    before = here[rows_at - HALO :]
                    acc = bias_bc_ref[side : side + 1, own] + here * taps[lag][None]
                    for k in range(lag):
                        first = HALO - lag + k
                        acc = acc + window[first : first + rows_at] * taps[k][None]
                    write(r, rows_at, silu(acc))

    def join(c, carry):
        onward(c).wait_recv()
        got = came[c]
        fades = exact_dot(fade_ref[...], spread_of(c))
        mine = sent[c].astype(F32)
        sent[c] = (fades[spans : spans + 1] * got.astype(F32) + mine).astype(BF16)

        @pl.when(me < n - 1)
        def _():
            onward(c).start()

        @pl.when(me == n - 1)
        def _():
            lax.fori_loop(0, n - 1, lambda q, z: (handed(q, c).start(), z)[1], 0)

        return carry

    base = jnp.where(me == 1, 2, chunks - 3 + me)
    first = jnp.clip(s - base, 0, chunks)
    stop = jnp.where(s == last_step, chunks, jnp.clip(s - base + 1, 0, chunks))
    stop = jnp.where(me == 0, first, stop)
    lax.fori_loop(first, stop, join, 0)

    low = lax.broadcasted_iota(jnp.int32, (SPAN, 2 * HEAD_DIM), 1) < HEAD_DIM
    pairs = HEADS_CHUNK // 2

    def pair_lanes(pair):
        return slice(pair * 2 * HEAD_DIM, (pair + 1) * 2 * HEAD_DIM)

    def pair_wide(ref, c, at, pair):
        return jnp.where(
            low, ref[c, at, 2 * pair : 2 * pair + 1], ref[c, at, 2 * pair + 1 : 2 * pair + 2]
        )

    @pl.when(s < chunks)
    def _():
        j = s
        bt = bt_ref.at[j // per]
        taps = taps_ref[...].astype(F32)
        before = edge_x[:, pl.ds(pl.multiple_of(j * CHUNK, CHUNK), CHUNK)].astype(F32)[EDGE - HALO :]
        fades = exact_dot(fade_ref[...], spread_of(j))

        def write(r, size, value):
            xc[j, r : r + size] = value.astype(BF16)

        conv_rows(lambda r, size: x_ref[r : r + size], before, taps, bias_ref[...], rows, write)
        state = None
        for k in range(spans):
            at = slice(k * SPAN, (k + 1) * SPAN)
            x_span = xc[j, at].astype(F32)
            scaled = jnp.concatenate(
                [
                    (x_span[:, pair_lanes(pair)] * pair_wide(tail_ref, j, at, pair)).astype(BF16)
                    for pair in range(pairs)
                ],
                axis=1,
            )
            part = dot(bt[:, at], scaled)
            state = part if state is None else fades[k : k + 1] * state + part
            if k < spans - 1:
                local[j, k] = state.astype(BF16)
        sent[j] = state.astype(BF16)

        @pl.when(me == 0)
        def _():
            onward(j).start()

    @pl.when(s >= lead)
    def _():
        j = s - lead
        fades = exact_dot(fade_ref[...], spread_of(j))
        g = j // per
        causal = lax.broadcasted_iota(jnp.int32, (SPAN, SPAN), 0) >= lax.broadcasted_iota(
            jnp.int32, (SPAN, SPAN), 1
        )
        none = jnp.zeros((), BF16)
        head_rows = pl.ds(pl.multiple_of(j * HEADS_CHUNK, HEADS_CHUNK), HEADS_CHUNK)
        for k in range(spans):
            at = slice(k * SPAN, (k + 1) * SPAN)
            c_span = c_ref[g, at]
            scores = dot(c_span, bt_ref[g, :, at])
            row_span = row_ref[head_rows, at]
            if k == 0:
                state = came[j]
            else:
                faded = jnp.broadcast_to(fades[spans + 2 + k : spans + 3 + k], (STATE, CHUNK)).astype(BF16)
                state = local[j, k - 1] + faded * came[j]
            readout = dot(c_span, state)
            for pair in range(pairs):
                lanes = pair_lanes(pair)
                weights = []
                for h in (2 * pair, 2 * pair + 1):
                    spacing = col_ref[j, at, h : h + 1] - row_span[h : h + 1]
                    decay = jnp.exp2(jnp.where(causal, spacing, -jnp.inf))
                    weights.append((decay * scores).astype(BF16))
                x_pair = xc[j, at, lanes]
                stacked = jnp.concatenate(
                    [jnp.where(low, x_pair, none), jnp.where(low, none, x_pair)], axis=0
                )
                within = dot(jnp.concatenate(weights, axis=1), stacked)
                out = (
                    within
                    + x_pair.astype(F32) * fades[spans + 1 : spans + 2, lanes]
                    + pair_wide(entry_ref, j, at, pair) * readout[:, lanes]
                )
                y_ref[at, lanes] = (out * silu(z_ref[at, lanes].astype(F32))).astype(BF16)

    @pl.when(s == last_step)
    def _():
        @pl.when(me < n - 1)
        def _():
            for copy in edge_copies():
                copy.wait_send()
            for c in range(chunks):
                onward(c).wait_send()
            for c in range(chunks):
                handed(0, c).wait_recv()
                final_out[:, c * CHUNK : (c + 1) * CHUNK] = piece[c]

        @pl.when(me == n - 1)
        def _():
            for c in range(chunks):
                lax.fori_loop(0, n - 1, lambda q, z: (handed(q, c).wait_send(), z)[1], 0)
                final_out[:, c * CHUNK : (c + 1) * CHUNK] = sent[c, (n - 1) * share :]


def scan(n, x, taps, bias, bc, taps_bc, bias_bc, dt, dt_bias, a_log, skip, z):
    rows, channels = x.shape
    chunks = channels // CHUNK
    heads = dt.shape[0]
    lead = leading(n, chunks)
    width = bc.shape[1]
    groups = width // (2 * STATE)
    share = STATE // n
    spans = rows // SPAN
    turn = lambda s: (0, jnp.minimum(s, chunks - 1))
    later = lambda s: (0, jnp.maximum(s - lead, 0))
    still = lambda s: (0, 0)
    return pl.pallas_call(
        functools.partial(scan_kernel, n),
        grid=(lead + chunks,),
        in_specs=[
            pl.BlockSpec((rows, CHUNK), turn),
            pl.BlockSpec((taps.shape[0], CHUNK), turn),
            pl.BlockSpec((1, CHUNK), turn),
            pl.BlockSpec((rows, width), still),
            pl.BlockSpec(taps_bc.shape, lambda s: (0, 0, 0)),
            pl.BlockSpec(bias_bc.shape, still),
            pl.BlockSpec((heads, rows), still),
            pl.BlockSpec((1, heads), still),
            pl.BlockSpec((1, heads), still),
            pl.BlockSpec((1, heads), still),
            pl.BlockSpec((rows, CHUNK), later),
            pl.BlockSpec(memory_space=pl.ANY),
            pl.BlockSpec(memory_space=pl.ANY),
        ],
        out_specs=[
            pl.BlockSpec((rows, CHUNK), later),
            pl.BlockSpec((share, channels), still),
        ],
        out_shape=[
            jax.ShapeDtypeStruct((rows, channels), BF16),
            jax.ShapeDtypeStruct((share, channels), BF16),
        ],
        scratch_shapes=[
            pltpu.VMEM((chunks, rows, CHUNK), BF16),
            pltpu.VMEM((chunks, STATE, CHUNK), BF16),
            pltpu.VMEM((chunks, STATE, CHUNK), BF16),
            pltpu.VMEM((chunks, share, CHUNK), BF16),
            pltpu.VMEM((chunks, spans - 1, STATE, CHUNK), BF16),
            pltpu.VMEM((chunks, rows, HEADS_CHUNK), F32),
            pltpu.VMEM((heads, rows), F32),
            pltpu.VMEM((chunks, rows, HEADS_CHUNK), F32),
            pltpu.VMEM((chunks, rows, HEADS_CHUNK), F32),
            pltpu.VMEM((-(-(2 * spans + 2) // 8) * 8, heads), F32),
            pltpu.VMEM((groups, STATE, rows), BF16),
            pltpu.VMEM((groups, rows, STATE), BF16),
            pltpu.VMEM((EDGE, channels), BF16),
            pltpu.VMEM((EDGE, width), BF16),
            pltpu.SemaphoreType.DMA((chunks,)),
            pltpu.SemaphoreType.DMA((chunks,)),
            pltpu.SemaphoreType.DMA((n - 1, chunks)),
            pltpu.SemaphoreType.DMA((chunks,)),
            pltpu.SemaphoreType.DMA((2,)),
            pltpu.SemaphoreType.DMA((2,)),
        ],
        compiler_params=pltpu.CompilerParams(
            dimension_semantics=("arbitrary",),
            vmem_limit_bytes=56 << 20,
            collective_id=0,
            has_side_effects=True,
        ),
        cost_estimate=pl.CostEstimate(
            flops=20 * rows * channels * STATE, bytes_accessed=4 * rows * channels, transcendentals=4 * rows * channels
        ),
    )(x, taps, bias, bc, taps_bc, bias_bc, dt, dt_bias, a_log, skip, z, x, bc)


def per_device(
    x_in,
    bc_in,
    z_in,
    dt_raw,
    conv_x,
    conv_bc,
    conv_bias_x,
    conv_bias_bc,
    dt_bias,
    a_log,
    d_skip,
    norm_gain,
):
    rows, channels = x_in.shape
    heads = dt_raw.shape[1]
    n = lax.axis_size("ctx")
    width = 2 * bc_in.shape[2]
    gated, final = scan(
        n,
        x_in,
        conv_x,
        conv_bias_x[None],
        bc_in.reshape(rows, width),
        conv_bc,
        conv_bias_bc,
        dt_raw.T,
        dt_bias[None],
        a_log[None],
        d_skip[None],
        z_in,
    )
    mixed = normed(gated, norm_gain[None], bc_in.shape[2] // STATE)
    share = STATE // n
    final_share = final.astype(F32).reshape(share, heads, HEAD_DIM).transpose(1, 2, 0)
    return (mixed, final_share)


def solution(mesh):
    in_specs = (
        P(("group", "ctx"), "tp"),
        P(("group", "ctx"), None, "tp"),
        P(("group", "ctx"), "tp"),
        P(("group", "ctx"), "tp"),
        P(None, "tp"),
        P(None, None, "tp"),
        P("tp"),
        P(None, "tp"),
        P("tp"),
        P("tp"),
        P("tp"),
        P("tp"),
    )
    out_specs = (P(("group", "ctx"), "tp"), P(("group", "tp"), None, "ctx"))
    return jax.shard_map(
        per_device, mesh=mesh, in_specs=in_specs, out_specs=out_specs, check_vma=False
    )
```

```python
import functools
import math

import jax
import jax.numpy as jnp
from jax import lax
from jax.experimental import pallas as pl
from jax.experimental.pallas import tpu as pltpu
from jax.sharding import PartitionSpec as P

HEAD_DIM = 64
STATE = 256
SPAN = 128
CHUNK = 512
HEADS_CHUNK = CHUNK // HEAD_DIM
HALO = 8
LOG2E = math.log2(math.e)

eps = 1e-05
F32 = jnp.float32
BF16 = jnp.bfloat16


def silu(v):
    half = 0.5 * v
    return half * jnp.tanh(half) + half


def dot(a, b):
    return jnp.dot(a, b, preferred_element_type=F32)


def params():
    return pltpu.CompilerParams(
        dimension_semantics=("arbitrary",), vmem_limit_bytes=48 << 20
    )


def norm_kernel(gated_ref, gain_ref, out_ref):
    gated = gated_ref[...].astype(F32)
    meansq = jnp.mean(gated * gated, axis=-1, keepdims=True)
    out_ref[...] = (gated * lax.rsqrt(meansq + eps) * gain_ref[...]).astype(BF16)


def normed(gated, gain, groups):
    rows, channels = gated.shape
    width = channels // groups
    size = 2 * SPAN
    blocks = rows // size
    block = pl.BlockSpec((size, width), lambda j: (j % blocks, j // blocks))
    return pl.pallas_call(
        norm_kernel,
        grid=(groups * blocks,),
        in_specs=[block, pl.BlockSpec((1, width), lambda j: (0, j // blocks))],
        out_specs=block,
        out_shape=jax.ShapeDtypeStruct((rows, channels), BF16),
        compiler_params=params(),
        cost_estimate=pl.CostEstimate(
            flops=4 * rows * channels, bytes_accessed=4 * rows * channels, transcendentals=rows
        ),
    )(gated, gain)


EDGE = 16
MESH = pl.DeviceIdType.MESH


def conv_rows(read, before, taps, bias, rows, write):
    step = 64
    lag = taps.shape[0] - 1
    for r in range(0, rows, step):
        here = read(r, step).astype(F32)
        window = jnp.concatenate([before, here], axis=0)
        before = here[step - HALO :]
        acc = bias + here * taps[lag][None]
        for k in range(lag):
            at = HALO - lag + k
            acc = acc + window[at : at + step] * taps[k][None]
        write(r, step, silu(acc))


def leading(n, chunks):
    return chunks + max(0, n - 4)


def three_terms(a):
    high = a.astype(BF16)
    rest = a - high.astype(F32)
    middle = rest.astype(BF16)
    return jnp.concatenate([high, middle, (rest - middle.astype(F32)).astype(BF16)], axis=0)


def exact_dot(a, b):
    return jnp.dot(a, b, preferred_element_type=F32, precision=lax.Precision.HIGHEST)


def scan_kernel(
    n,
    x_ref,
    taps_ref,
    bias_ref,
    bc_ref,
    taps_bc_ref,
    bias_bc_ref,
    dt_ref,
    dt_bias_ref,
    a_log_ref,
    skip_ref,
    z_ref,
    x_any,
    bc_any,
    y_ref,
    final_out,
    xc,
    sent,
    came,
    piece,
    local,
    col_ref,
    row_ref,
    tail_ref,
    entry_ref,
    fade_ref,
    fade_terms,
    bt_ref,
    c_ref,
    edge_x,
    edge_bc,
    send_sem,
    recv_sem,
    piece_send,
    piece_recv,
    edge_send,
    edge_recv,
):
    s = pl.program_id(0)
    chunks = sent.shape[0]
    lead = leading(n, chunks)
    last_step = lead + chunks - 1
    me = lax.axis_index("ctx")
    rows = x_ref.shape[0]
    spans = rows // SPAN
    heads = dt_ref.shape[0]
    groups = bt_ref.shape[0]
    per = chunks // groups
    share = STATE // n
    right = jnp.minimum(me + 1, n - 1)

    def edge_copies():
        return [
            pltpu.make_async_remote_copy(
                src_ref=whole.at[pl.ds(rows - EDGE, EDGE)],
                dst_ref=edge,
                send_sem=edge_send.at[i],
                recv_sem=edge_recv.at[i],
                device_id={"ctx": right},
                device_id_type=MESH,
            )
            for i, (whole, edge) in enumerate(((bc_any, edge_bc), (x_any, edge_x)))
        ]

    def onward(c):
        return pltpu.make_async_remote_copy(
            src_ref=sent.at[c],
            dst_ref=came.at[c],
            send_sem=send_sem.at[c],
            recv_sem=recv_sem.at[c],
            device_id={"ctx": right},
            device_id_type=MESH,
        )

    def handed(q, c):
        return pltpu.make_async_remote_copy(
            src_ref=sent.at[c, pl.ds(pl.multiple_of(q * share, share), share)],
            dst_ref=piece.at[c],
            send_sem=piece_send.at[q, c],
            recv_sem=piece_recv.at[c],
            device_id={"ctx": q},
            device_id_type=MESH,
        )

    def spread_of(c):
        shape = (heads, CHUNK)
        return (
            lax.broadcasted_iota(jnp.int32, shape, 1) // HEAD_DIM + c * HEADS_CHUNK
            == lax.broadcasted_iota(jnp.int32, shape, 0)
        ).astype(BF16)

    def fades_of(c):
        terms = dot(fade_terms[...], spread_of(c))
        size = terms.shape[0] // 3
        return terms[:size] + terms[size : 2 * size] + terms[2 * size :]

    def span_sums(k):
        at = slice(k * SPAN, (k + 1) * SPAN)
        rate = -LOG2E * jnp.exp(a_log_ref[...])
        lower = (
            lax.broadcasted_iota(jnp.int32, (SPAN, SPAN), 0)
            >= lax.broadcasted_iota(jnp.int32, (SPAN, SPAN), 1)
        ).astype(F32)
        v = dt_ref[:, at].T + dt_bias_ref[...]
        step = jnp.maximum(v, 0.0) + jnp.log1p(jnp.exp(-jnp.abs(v)))
        return at, step, exact_dot(lower, step * rate)

    def conv_bc(side):
        for g in range(groups):
            lanes = slice((side * groups + g) * STATE, (side * groups + g + 1) * STATE)
            own = slice(g * STATE, (g + 1) * STATE)
            lag = taps_bc_ref.shape[0] - 1
            before = edge_bc[:, lanes].astype(F32)[EDGE - HALO :]
            taps = taps_bc_ref[:, side, own].astype(F32)
            for r in range(0, rows, SPAN):
                here = bc_ref[r : r + SPAN, lanes].astype(F32)
                window = jnp.concatenate([before, here], axis=0)
                before = here[SPAN - HALO :]
                acc = bias_bc_ref[side : side + 1, own] + here * taps[lag][None]
                for k in range(lag):
                    first = HALO - lag + k
                    acc = acc + window[first : first + SPAN] * taps[k][None]
                value = silu(acc).astype(BF16)
                if side == 0:
                    bt_ref[g, :, r : r + SPAN] = value.astype(F32).T.astype(BF16)
                else:
                    c_ref[g, r : r + SPAN] = value

    @pl.when(s == 0)
    def _():
        barrier = pltpu.get_barrier_semaphore()
        for k in range(1, n):
            pl.semaphore_signal(
                barrier, inc=1, device_id={"ctx": lax.rem(me + k, n)}, device_id_type=MESH
            )
        pl.semaphore_wait(barrier, n - 1)

        @pl.when(me < n - 1)
        def _():
            for copy in edge_copies():
                copy.start()

        so_far = jnp.zeros((1, heads), F32)
        for k in range(spans):
            at, step, cumul = span_sums(k)
            last = cumul[SPAN - 1 :]
            tail = jnp.exp2(last - cumul) * step
            for c in range(chunks):
                tail_ref[c, at] = tail[:, c * HEADS_CHUNK : (c + 1) * HEADS_CHUNK]
            fade_ref[k : k + 1] = jnp.exp2(last)
            fade_ref[spans + 2 + k : spans + 3 + k] = jnp.exp2(so_far)
            so_far = so_far + last
        fade_ref[spans : spans + 1] = jnp.exp2(so_far)
        fade_ref[spans + 1 : spans + 2] = skip_ref[...]
        if fade_ref.shape[0] > 2 * spans + 2:
            fade_ref[2 * spans + 2 :] = jnp.zeros((fade_ref.shape[0] - 2 * spans - 2, heads), F32)

        fade_terms[...] = three_terms(fade_ref[...])

        @pl.when(me == 0)
        def _():
            edge_x[...] = jnp.zeros_like(edge_x)
            edge_bc[...] = jnp.zeros_like(edge_bc)
            came[...] = jnp.zeros_like(came)

        @pl.when(me > 0)
        def _():
            for copy in edge_copies():
                copy.wait_recv()

        conv_bc(0)

    @pl.when(s == 1)
    def _():
        for k in range(spans):
            at, step, cumul = span_sums(k)
            entry = jnp.exp2(cumul)
            for c in range(chunks):
                mine = slice(c * HEADS_CHUNK, (c + 1) * HEADS_CHUNK)
                col_ref[c, at] = cumul[:, mine]
                entry_ref[c, at] = entry[:, mine]
            rowed = cumul - jnp.log2(step)
            wide = jnp.concatenate([rowed] * (128 // heads), axis=1) if heads < 128 else rowed
            row_ref[:, at] = wide.T[:heads]
        conv_bc(1)

    def join(c, carry):
        onward(c).wait_recv()
        got = came[c]
        fades = fades_of(c)
        mine = sent[c].astype(F32)
        sent[c] = (fades[spans : spans + 1] * got.astype(F32) + mine).astype(BF16)

        @pl.when(me < n - 1)
        def _():
            onward(c).start()

        @pl.when(me == n - 1)
        def _():
            lax.fori_loop(0, n - 1, lambda q, z: (handed(q, c).start(), z)[1], 0)

        return carry

    base = jnp.where(me == 1, 2, chunks - 3 + me)
    first = jnp.clip(s - base, 0, chunks)
    stop = jnp.where(s == last_step, chunks, jnp.clip(s - base + 1, 0, chunks))
    stop = jnp.where(me == 0, first, stop)
    lax.fori_loop(first, stop, join, 0)

    low = lax.broadcasted_iota(jnp.int32, (SPAN, 2 * HEAD_DIM), 1) < HEAD_DIM
    pairs = HEADS_CHUNK // 2

    def pair_lanes(pair):
        return slice(pair * 2 * HEAD_DIM, (pair + 1) * 2 * HEAD_DIM)

    def pair_wide(ref, c, at, pair):
        return jnp.where(
            low, ref[c, at, 2 * pair : 2 * pair + 1], ref[c, at, 2 * pair + 1 : 2 * pair + 2]
        )

    @pl.when(s < chunks)
    def _():
        j = s
        bt = bt_ref.at[j // per]
        taps = taps_ref[...].astype(F32)
        before = edge_x[:, pl.ds(pl.multiple_of(j * CHUNK, CHUNK), CHUNK)].astype(F32)[EDGE - HALO :]
        fades = fades_of(j)

        def write(r, size, value):
            xc[j, r : r + size] = value.astype(BF16)

        conv_rows(lambda r, size: x_ref[r : r + size], before, taps, bias_ref[...], rows, write)
        state = None
        for k in range(spans):
            at = slice(k * SPAN, (k + 1) * SPAN)
            x_span = xc[j, at].astype(F32)
            scaled = jnp.concatenate(
                [
                    (x_span[:, pair_lanes(pair)] * pair_wide(tail_ref, j, at, pair)).astype(BF16)
                    for pair in range(pairs)
                ],
                axis=1,
            )
            part = dot(bt[:, at], scaled)
            state = part if state is None else fades[k : k + 1] * state + part
            if k < spans - 1:
                local[j, k] = state.astype(BF16)
        sent[j] = state.astype(BF16)

        @pl.when(me == 0)
        def _():
            onward(j).start()

    @pl.when(s >= lead)
    def _():
        j = s - lead
        fades = fades_of(j)
        g = j // per
        causal = lax.broadcasted_iota(jnp.int32, (SPAN, SPAN), 0) >= lax.broadcasted_iota(
            jnp.int32, (SPAN, SPAN), 1
        )
        none = jnp.zeros((), BF16)
        head_rows = pl.ds(pl.multiple_of(j * HEADS_CHUNK, HEADS_CHUNK), HEADS_CHUNK)
        for k in range(spans):
            at = slice(k * SPAN, (k + 1) * SPAN)
            c_span = c_ref[g, at]
            scores = dot(c_span, bt_ref[g, :, at])
            row_span = row_ref[head_rows, at]
            if k == 0:
                state = came[j]
            else:
                faded = jnp.broadcast_to(fades[spans + 2 + k : spans + 3 + k], (STATE, CHUNK)).astype(BF16)
                state = local[j, k - 1] + faded * came[j]
            readout = dot(c_span, state)
            for pair in range(pairs):
                lanes = pair_lanes(pair)
                weights = []
                for h in (2 * pair, 2 * pair + 1):
                    spacing = col_ref[j, at, h : h + 1] - row_span[h : h + 1]
                    decay = jnp.exp2(jnp.where(causal, spacing, -jnp.inf))
                    weights.append((decay * scores).astype(BF16))
                x_pair = xc[j, at, lanes]
                stacked = jnp.concatenate(
                    [jnp.where(low, x_pair, none), jnp.where(low, none, x_pair)], axis=0
                )
                within = dot(jnp.concatenate(weights, axis=1), stacked)
                out = (
                    within
                    + x_pair.astype(F32) * fades[spans + 1 : spans + 2, lanes]
                    + pair_wide(entry_ref, j, at, pair) * readout[:, lanes]
                )
                y_ref[at, lanes] = (out * silu(z_ref[at, lanes].astype(F32))).astype(BF16)

    @pl.when(s == last_step)
    def _():
        @pl.when(me < n - 1)
        def _():
            for copy in edge_copies():
                copy.wait_send()
            for c in range(chunks):
                onward(c).wait_send()
            for c in range(chunks):
                handed(0, c).wait_recv()
                final_out[:, c * CHUNK : (c + 1) * CHUNK] = piece[c]

        @pl.when(me == n - 1)
        def _():
            for c in range(chunks):
                lax.fori_loop(0, n - 1, lambda q, z: (handed(q, c).wait_send(), z)[1], 0)
                final_out[:, c * CHUNK : (c + 1) * CHUNK] = sent[c, (n - 1) * share :]


def scan(n, x, taps, bias, bc, taps_bc, bias_bc, dt, dt_bias, a_log, skip, z):
    rows, channels = x.shape
    chunks = channels // CHUNK
    heads = dt.shape[0]
    lead = leading(n, chunks)
    width = bc.shape[1]
    groups = width // (2 * STATE)
    share = STATE // n
    spans = rows // SPAN
    turn = lambda s: (0, jnp.minimum(s, chunks - 1))
    later = lambda s: (0, jnp.maximum(s - lead, 0))
    still = lambda s: (0, 0)
    return pl.pallas_call(
        functools.partial(scan_kernel, n),
        grid=(lead + chunks,),
        in_specs=[
            pl.BlockSpec((rows, CHUNK), turn),
            pl.BlockSpec((taps.shape[0], CHUNK), turn),
            pl.BlockSpec((1, CHUNK), turn),
            pl.BlockSpec((rows, width), still),
            pl.BlockSpec(taps_bc.shape, lambda s: (0, 0, 0)),
            pl.BlockSpec(bias_bc.shape, still),
            pl.BlockSpec((heads, rows), still),
            pl.BlockSpec((1, heads), still),
            pl.BlockSpec((1, heads), still),
            pl.BlockSpec((1, heads), still),
            pl.BlockSpec((rows, CHUNK), later),
            pl.BlockSpec(memory_space=pl.ANY),
            pl.BlockSpec(memory_space=pl.ANY),
        ],
        out_specs=[
            pl.BlockSpec((rows, CHUNK), later),
            pl.BlockSpec((share, channels), still),
        ],
        out_shape=[
            jax.ShapeDtypeStruct((rows, channels), BF16),
            jax.ShapeDtypeStruct((share, channels), BF16),
        ],
        scratch_shapes=[
            pltpu.VMEM((chunks, rows, CHUNK), BF16),
            pltpu.VMEM((chunks, STATE, CHUNK), BF16),
            pltpu.VMEM((chunks, STATE, CHUNK), BF16),
            pltpu.VMEM((chunks, share, CHUNK), BF16),
            pltpu.VMEM((chunks, spans - 1, STATE, CHUNK), BF16),
            pltpu.VMEM((chunks, rows, HEADS_CHUNK), F32),
            pltpu.VMEM((heads, rows), F32),
            pltpu.VMEM((chunks, rows, HEADS_CHUNK), F32),
            pltpu.VMEM((chunks, rows, HEADS_CHUNK), F32),
            pltpu.VMEM((-(-(2 * spans + 2) // 16) * 16, heads), F32),
            pltpu.VMEM((-(-(2 * spans + 2) // 16) * 48, heads), BF16),
            pltpu.VMEM((groups, STATE, rows), BF16),
            pltpu.VMEM((groups, rows, STATE), BF16),
            pltpu.VMEM((EDGE, channels), BF16),
            pltpu.VMEM((EDGE, width), BF16),
            pltpu.SemaphoreType.DMA((chunks,)),
            pltpu.SemaphoreType.DMA((chunks,)),
            pltpu.SemaphoreType.DMA((n - 1, chunks)),
            pltpu.SemaphoreType.DMA((chunks,)),
            pltpu.SemaphoreType.DMA((2,)),
            pltpu.SemaphoreType.DMA((2,)),
        ],
        compiler_params=pltpu.CompilerParams(
            dimension_semantics=("arbitrary",),
            vmem_limit_bytes=56 << 20,
            collective_id=0,
            has_side_effects=True,
        ),
        cost_estimate=pl.CostEstimate(
            flops=20 * rows * channels * STATE, bytes_accessed=4 * rows * channels, transcendentals=4 * rows * channels
        ),
    )(x, taps, bias, bc, taps_bc, bias_bc, dt, dt_bias, a_log, skip, z, x, bc)


def per_device(
    x_in,
    bc_in,
    z_in,
    dt_raw,
    conv_x,
    conv_bc,
    conv_bias_x,
    conv_bias_bc,
    dt_bias,
    a_log,
    d_skip,
    norm_gain,
):
    rows, channels = x_in.shape
    heads = dt_raw.shape[1]
    n = lax.axis_size("ctx")
    width = 2 * bc_in.shape[2]
    gated, final = scan(
        n,
        x_in,
        conv_x,
        conv_bias_x[None],
        bc_in.reshape(rows, width),
        conv_bc,
        conv_bias_bc,
        dt_raw.T,
        dt_bias[None],
        a_log[None],
        d_skip[None],
        z_in,
    )
    mixed = normed(gated, norm_gain[None], bc_in.shape[2] // STATE)
    share = STATE // n
    final_share = final.astype(F32).reshape(share, heads, HEAD_DIM).transpose(1, 2, 0)
    return (mixed, final_share)


def solution(mesh):
    in_specs = (
        P(("group", "ctx"), "tp"),
        P(("group", "ctx"), None, "tp"),
        P(("group", "ctx"), "tp"),
        P(("group", "ctx"), "tp"),
        P(None, "tp"),
        P(None, None, "tp"),
        P("tp"),
        P(None, "tp"),
        P("tp"),
        P("tp"),
        P("tp"),
        P("tp"),
    )
    out_specs = (P(("group", "ctx"), "tp"), P(("group", "tp"), None, "ctx"))
    return jax.shard_map(
        per_device, mesh=mesh, in_specs=in_specs, out_specs=out_specs, check_vma=False
    )
```
